512 devices in a mesh: dp: 32 (over y, z_lo, core), ctx: 16 (over x, z_hi).
Axes of the slice: x: 4, y: 8, z: 8 (z_hi: 4, z_lo: 2; z = z_hi * 2 + z_lo), core: 2. Of those that a mesh axis runs over, the one named last changes fastest.
Arguments:
- queries: bfloat16 [32, 2048, 2048], P('dp', 'ctx'), may hold values from -21 to 21
- keys: bfloat16 [32, 2048, 512], P('dp', 'ctx'), may hold values from -21 to 21
- values: bfloat16 [32, 2048, 512], P('dp', 'ctx'), may hold values from -6 to 6
- dout: bfloat16 [32, 2048, 2048], P('dp', 'ctx'), may hold values from -6 to 6
- sinks: float32 [16], replicated, may hold values from 0 to 6
Outputs:
- grad_queries: bfloat16 [32, 2048, 2048], P('dp', 'ctx')
- grad_keys: bfloat16 [32, 2048, 512], P('dp', 'ctx')
- grad_values: bfloat16 [32, 2048, 512], P('dp', 'ctx')
- sink_grad: float32 [16], replicated
The draws below stay inside these ranges and needn't reach their ends.
All inputs are finite; a program needn't handle non-finite values.
Results may differ from the reference program's by a relative error of at most 0.03.
Values may be sent and summed in bfloat16 or wider, within the bound.
A program may use at most 64 MiB of HBM per device.

```python
import jax
import jax.numpy as jnp
from jax import lax

HEADS = 16
KV_HEADS = 4
HEAD = 128
WINDOW = 128
TOK_DEV = 128
BATCH = 32
LENGTH = 2048


def draw_queries(key, part):
    drawn = jnp.clip(jax.random.normal(jax.random.fold_in(key, 21), (BATCH, LENGTH, HEADS * HEAD), jnp.float32), -4.0, 4.0)
    return drawn.astype(jnp.bfloat16)


def draw_keys(key, part):
    drawn = jnp.clip(jax.random.normal(jax.random.fold_in(key, 22), (BATCH, LENGTH, KV_HEADS * HEAD), jnp.float32), -4.0, 4.0)
    return drawn.astype(jnp.bfloat16)


def block_levels(rng, dims, shards, least, high):
    gain, own = 1.0, jax.random.fold_in(rng, 6)
    for dim, shards_of in shards:
        heights = jnp.exp(jax.random.uniform(jax.random.fold_in(own, dim), (shards_of,), jnp.float32, least / len(shards), high / len(shards)))
        gain = gain * jnp.repeat(heights, dims[dim] // shards_of).reshape([-1 if axis == dim else 1 for axis in range(len(dims))])
    return gain


def gaussian(key, dims, width, limit, cuts=(), kind=jnp.bfloat16):
    drawn = jax.random.normal(key, dims, jnp.float32) * width
    if len(cuts) > 0:
        drawn = block_levels(key, dims, cuts, -0.22, 0.18) * drawn
    return jnp.clip(drawn, min=-limit, max=limit).astype(kind)


def setup_inputs(seed: int = 0) -> dict:
    key_list = jax.random.split(jax.random.key(seed), 6)
    return {
        "queries": draw_queries(jax.random.fold_in(key_list[5], 71), 0),
        "keys": draw_keys(jax.random.fold_in(key_list[5], 71), 0),
        "values": gaussian(key_list[2], (BATCH, LENGTH, KV_HEADS * HEAD), 1.0, 6.0, ((0, 32), (1, 16))),
        "dout": gaussian(key_list[3], (BATCH, LENGTH, HEADS * HEAD), 1.0, 6.0, ((0, 32), (1, 16))),
        "sinks": jnp.clip(jax.random.uniform(key_list[4], (HEADS,), jnp.float32, 0.0, 6.0), 0.0, 6.0),
    }


def block_terms(query_rows, key_rows, value_rows, grad_rows, sinks, allowed):
    group_size = HEADS // KV_HEADS
    row_count = query_rows.shape[0]
    key_count = key_rows.shape[0]
    score_scale = HEAD ** (-0.5)
    key_mask = jnp.broadcast_to(allowed[:, None, :], (row_count, group_size, key_count)).reshape(row_count * group_size, key_count)
    grad_query_list = []
    grad_key_list = []
    grad_value_list = []
    sink_list = []
    for kv_head in range(KV_HEADS):
        low = kv_head * group_size * HEAD
        high = (kv_head + 1) * group_size * HEAD
        query_group = query_rows[:, low:high].reshape(row_count * group_size, HEAD)
        grad_group = grad_rows[:, low:high].reshape(row_count * group_size, HEAD)
        key_group = key_rows[:, kv_head * HEAD:(kv_head + 1) * HEAD]
        value_group = value_rows[:, kv_head * HEAD:(kv_head + 1) * HEAD]
        scores = lax.dot_general(query_group, key_group, (((1,), (1,)), ((), ())), preferred_element_type=jnp.float32) * score_scale
        sink_rows = jnp.tile(sinks[kv_head * group_size:(kv_head + 1) * group_size], row_count)
        row_max = jnp.maximum(lax.optimization_barrier(jnp.max(jnp.where(key_mask, scores, -jnp.inf), axis=1)), sink_rows)
        weights = jnp.where(key_mask, jnp.exp(scores - row_max[:, None]), 0.0)
        row_total = jnp.exp(sink_rows - row_max) + lax.optimization_barrier(jnp.sum(weights, axis=1))
        log_total = row_max + jnp.log(row_total)
        probabilities = jnp.where(key_mask, jnp.exp(scores - log_total[:, None]), 0.0)
        probs_low = probabilities.astype(jnp.bfloat16)
        attended = jnp.dot(probs_low, value_group, preferred_element_type=jnp.float32).astype(jnp.bfloat16)
        attended = lax.optimization_barrier(attended)
        row_delta = lax.optimization_barrier(jnp.sum(grad_group.astype(jnp.float32) * attended.astype(jnp.float32), axis=1))
        grad_prob = lax.dot_general(grad_group, value_group, (((1,), (1,)), ((), ())), preferred_element_type=jnp.float32)
        dscore = (probabilities * (grad_prob - row_delta[:, None])).astype(jnp.bfloat16)
        grad_query = jnp.dot(dscore, key_group, preferred_element_type=jnp.float32) * score_scale
        grad_query_list.append(grad_query.reshape(row_count, group_size * HEAD))
        grad_key_list.append(lax.dot_general(dscore, query_group, (((0,), (0,)), ((), ())), preferred_element_type=jnp.float32) * score_scale)
        grad_value_list.append(lax.dot_general(probs_low, grad_group, (((0,), (0,)), ((), ())), preferred_element_type=jnp.float32))
        sink_list.append(-lax.optimization_barrier(jnp.sum((jnp.exp(sink_rows - log_total) * row_delta).reshape(row_count, group_size), axis=0)))
    return (jnp.concatenate(grad_query_list, axis=1), jnp.concatenate(grad_key_list, axis=1), jnp.concatenate(grad_value_list, axis=1), jnp.concatenate(sink_list, axis=0))

def reference(queries, keys, values, dout, sinks):
    block_count = LENGTH // TOK_DEV

    def per_sequence(inputs):
        seq_queries, seq_keys, seq_values, seq_grads = inputs
        padding = jnp.zeros((WINDOW, seq_keys.shape[1]), seq_keys.dtype)
        keys_padded = jnp.concatenate([padding, seq_keys], axis=0)
        values_padded = jnp.concatenate([padding, seq_values], axis=0)

        def block_step(carried, block_index):
            key_acc, value_acc, sink_acc = carried
            block_start = (block_index * TOK_DEV).astype(jnp.int32)
            query_rows = lax.dynamic_slice_in_dim(seq_queries, block_start, TOK_DEV, 0)
            grad_rows = lax.dynamic_slice_in_dim(seq_grads, block_start, TOK_DEV, 0)
            key_rows = lax.dynamic_slice_in_dim(keys_padded, block_start, WINDOW + TOK_DEV, 0)
            value_rows = lax.dynamic_slice_in_dim(values_padded, block_start, WINDOW + TOK_DEV, 0)
            query_pos = block_start + jnp.arange(TOK_DEV, dtype=jnp.int32)
            key_pos = block_start - WINDOW + jnp.arange(WINDOW + TOK_DEV, dtype=jnp.int32)
            allowed = (key_pos[None, :] <= query_pos[:, None]) & (key_pos[None, :] > query_pos[:, None] - WINDOW) & (key_pos[None, :] >= 0)
            grad_query, grad_key, grad_value, sink_term = block_terms(query_rows, key_rows, value_rows, grad_rows, sinks, allowed)
            key_acc = lax.dynamic_update_slice_in_dim(key_acc, lax.dynamic_slice_in_dim(key_acc, block_start, WINDOW + TOK_DEV, 0) + grad_key, block_start, 0)
            value_acc = lax.dynamic_update_slice_in_dim(value_acc, lax.dynamic_slice_in_dim(value_acc, block_start, WINDOW + TOK_DEV, 0) + grad_value, block_start, 0)
            return ((key_acc, value_acc, sink_acc + sink_term), grad_query.astype(jnp.bfloat16))
        start_acc = jnp.zeros((WINDOW + LENGTH, KV_HEADS * HEAD), jnp.float32)
        carried, query_blocks = lax.scan(block_step, (start_acc, start_acc, jnp.zeros((HEADS,), jnp.float32)), jnp.arange(block_count, dtype=jnp.int32))
        key_acc, value_acc, sink_acc = carried
        return (query_blocks.reshape(LENGTH, HEADS * HEAD), key_acc[WINDOW:].astype(jnp.bfloat16), value_acc[WINDOW:].astype(jnp.bfloat16), sink_acc)
    grad_queries, grad_keys, grad_values, sink_terms = lax.map(per_sequence, (queries, keys, values, dout))
    sink_grad = lax.optimization_barrier(jnp.sum(sink_terms, axis=0)) / jnp.sqrt(jnp.float32(BATCH * LENGTH))
    return (grad_queries, grad_keys, grad_values, sink_grad)
```

```python
import functools

import jax
import jax.numpy as jnp
from jax import lax
from jax.experimental import pallas as pl
from jax.experimental.pallas import tpu as pltpu
from jax.sharding import PartitionSpec as P

HEADS = 16
KV_HEADS = 4
GROUP = HEADS // KV_HEADS
HEAD = 128
TOK = 128
SCALE = HEAD ** (-0.5)
LOG2E = 1.4426950408889634
MASKED = -1e30
MESH = pl.DeviceIdType.MESH

NT = (((1,), (1,)), ((), ()))
NN = (((1,), (0,)), ((), ()))
TN = (((0,), (0,)), ((), ()))


def dot(a, b, dims):
    return lax.dot_general(a, b, dims, preferred_element_type=jnp.float32)


def kernel(
    nd, nc, token_root,
    q_hbm, k_hbm, v_hbm, do_hbm, sinks_hbm,
    dq_hbm, dk_hbm, dv_hbm, sg_ref,
    qv, dov, kj, vj, dqv, own, back, landed, outv, bias, sinks_s, terms, part_a, part_b,
    in_sem, kv_sem, sink_sem, halo_send, halo_recv, grad_send, grad_recv, dq_sem, out_sem,
    sum_send, sum_recv,
):
    d = lax.axis_index("dp")
    c = lax.axis_index("ctx")
    right = lax.rem(c + 1, nc)
    left = lax.rem(c + nc - 1, nc)

    def cols(h):
        return pl.ds(h * HEAD, HEAD)

    loads = []
    for g in range(KV_HEADS):
        pairs = [(k_hbm.at[0, :, cols(g)], kj.at[g, pl.ds(TOK, TOK)]), (v_hbm.at[0, :, cols(g)], vj.at[g, pl.ds(TOK, TOK)])]
        loads.append([pltpu.make_async_copy(s, t, kv_sem.at[g, n]) for n, (s, t) in enumerate(pairs)])
        for h in range(g * GROUP, (g + 1) * GROUP):
            loads[g].append(pltpu.make_async_copy(q_hbm.at[0, :, cols(h)], qv.at[h], in_sem.at[0, h]))
            loads[g].append(pltpu.make_async_copy(do_hbm.at[0, :, cols(h)], dov.at[h], in_sem.at[1, h]))
    sink_load = pltpu.make_async_copy(sinks_hbm, sinks_s, sink_sem)
    sink_load.start()
    for group in loads:
        for copy in group:
            copy.start()

    barrier = pltpu.get_barrier_semaphore()
    for step in range(1, nc):
        pl.semaphore_signal(barrier, inc=1, device_id=(d, lax.rem(c + step, nc)), device_id_type=MESH)
    for step in range(1, nd):
        pl.semaphore_signal(barrier, inc=1, device_id=(lax.rem(d + step, nd), c), device_id_type=MESH)
    pl.semaphore_wait(barrier, nc - 1 + nd - 1)

    def remote(src, dst, send, recv, device):
        return pltpu.make_async_remote_copy(
            src_ref=src, dst_ref=dst, send_sem=send, recv_sem=recv, device_id=device, device_id_type=MESH
        )

    halo = []
    for g in range(KV_HEADS):
        for n, (src, dst) in enumerate(((k_hbm, kj), (v_hbm, vj))):
            halo.append(
                remote(src.at[0, :, cols(g)], dst.at[g, pl.ds(0, TOK)], halo_send.at[g, n], halo_recv.at[g, n], (d, right))
            )
            halo[-1].start()

    key = lax.broadcasted_iota(jnp.int32, (TOK, TOK), 0)
    query = lax.broadcasted_iota(jnp.int32, (TOK, TOK), 1)
    first = jnp.where(c == 0, TOK, 0)
    bias[0:TOK] = jnp.where(key > query + first, 0.0, MASKED)
    bias[TOK:] = jnp.where(key <= query, 0.0, MASKED)
    sink_load.wait()

    grads = []
    for g in range(KV_HEADS):
        for copy in loads[g]:
            copy.wait()
        halo[2 * g].wait_recv()
        halo[2 * g + 1].wait_recv()
        heads = pl.ds(g * GROUP, GROUP)
        qs = qv[heads].reshape(GROUP * TOK, HEAD)
        dos = dov[heads].reshape(GROUP * TOK, HEAD)
        kk = kj[g]
        vv = vj[g]
        mask = bias[...]
        mask = jnp.concatenate([mask] * GROUP, axis=1)
        sink = jnp.concatenate(
            [jnp.full((1, TOK), sinks_s[g * GROUP + n] * LOG2E, jnp.float32) for n in range(GROUP)], axis=1
        )
        s = dot(kk, qs, NT) * (SCALE * LOG2E) + mask
        top = jnp.maximum(jnp.max(s, axis=0, keepdims=True), sink)
        e = jnp.exp2(s - top)
        at_sink = jnp.exp2(sink - top)
        inv = 1.0 / (jnp.sum(e, axis=0, keepdims=True) + at_sink)
        p = e * inv
        dp = dot(vv, dos, NT)
        weighted = p * dp
        delta = jnp.sum(weighted, axis=0, keepdims=True)
        term = at_sink * inv * delta
        for n in range(GROUP):
            terms[pl.ds(g * GROUP + n, 1), :] = term[:, n * TOK : (n + 1) * TOK]
        ds = (weighted - p * delta).astype(jnp.bfloat16)
        pr = p.astype(jnp.bfloat16)
        dk = dot(ds, qs, NN) * SCALE
        dv = dot(pr, dos, NN)
        back[0, g] = dk[:TOK].astype(jnp.bfloat16)
        back[1, g] = dv[:TOK].astype(jnp.bfloat16)
        own[0, g] = dk[TOK:]
        own[1, g] = dv[TOK:]
        dq = dot(ds, kk, TN) * SCALE
        dqv[heads] = dq.astype(jnp.bfloat16).reshape(GROUP, TOK, HEAD)
        if g == KV_HEADS - 1:
            row = lax.broadcasted_iota(jnp.int32, (HEADS, TOK), 0)
            lane = lax.broadcasted_iota(jnp.int32, (HEADS, TOK), 1)
            sums = jnp.sum(terms[...], axis=1, keepdims=True)
            part_a[d] = jnp.sum(jnp.where(row == lane, sums, 0.0), axis=0, keepdims=True)
            stage_a = [
                remote(part_a.at[d], part_a.at[d], sum_send.at[0], sum_recv.at[0], (lax.rem(d + step, nd), c))
                for step in range(1, nd)
            ]
            for copy in stage_a:
                copy.start()
        for n in range(2):
            copy = remote(back.at[n, g], landed.at[n, g], grad_send.at[g, n], grad_recv.at[g, n], (d, left))
            copy.start()
            grads.append(copy)
        for h in range(g * GROUP, (g + 1) * GROUP):
            pltpu.make_async_copy(dqv.at[h], dq_hbm.at[0, :, cols(h)], dq_sem.at[h]).start()

    remote(part_a.at[pl.ds(0, nd - 1)], part_a.at[pl.ds(0, nd - 1)], sum_send.at[0], sum_recv.at[0], (d, left)).wait_recv()
    part_b[c] = jnp.sum(part_a[...], axis=0)
    for step in range(1, nc):
        remote(part_b.at[c], part_b.at[c], sum_send.at[1], sum_recv.at[1], (d, lax.rem(c + step, nc))).start()

    for g in range(KV_HEADS):
        for n, out in enumerate((dk_hbm, dv_hbm)):
            grads[2 * g + n].wait_recv()
            outv[n, g] = (own[n, g] + landed[n, g].astype(jnp.float32)).astype(jnp.bfloat16)
            pltpu.make_async_copy(outv.at[n, g], out.at[0, :, cols(g)], out_sem.at[g, n]).start()

    remote(part_b.at[pl.ds(0, nc - 1)], part_b.at[pl.ds(0, nc - 1)], sum_send.at[1], sum_recv.at[1], (d, left)).wait_recv()
    sg_ref[...] = jnp.sum(part_b[...], axis=0) * (-1.0 / token_root)

    for copy in halo + grads:
        copy.wait_send()
    remote(part_a.at[pl.ds(0, nd - 1)], part_a.at[pl.ds(0, nd - 1)], sum_send.at[0], sum_recv.at[0], (d, left)).wait_send()
    remote(part_b.at[pl.ds(0, nc - 1)], part_b.at[pl.ds(0, nc - 1)], sum_send.at[1], sum_recv.at[1], (d, left)).wait_send()
    for h in range(HEADS):
        pltpu.make_async_copy(dqv.at[h], dq_hbm.at[0, :, cols(h)], dq_sem.at[h]).wait()
    for g in range(KV_HEADS):
        for n, out in enumerate((dk_hbm, dv_hbm)):
            pltpu.make_async_copy(outv.at[n, g], out.at[0, :, cols(g)], out_sem.at[g, n]).wait()


def solution(mesh):
    nd, nc = mesh.shape["dp"], mesh.shape["ctx"]
    any_space = pl.BlockSpec(memory_space=pl.ANY)

    def body(queries, keys, values, dout, sinks):
        token_root = float(nd * queries.shape[0] * nc * queries.shape[1]) ** 0.5
        bf16, f32 = jnp.bfloat16, jnp.float32
        dq, dk, dv, sg = pl.pallas_call(
            functools.partial(kernel, nd, nc, token_root),
            out_shape=(
                jax.ShapeDtypeStruct(queries.shape, bf16),
                jax.ShapeDtypeStruct(keys.shape, bf16),
                jax.ShapeDtypeStruct(values.shape, bf16),
                jax.ShapeDtypeStruct((1, HEAD), f32),
            ),
            in_specs=[any_space] * 5,
            out_specs=(any_space, any_space, any_space, pl.BlockSpec(memory_space=pltpu.VMEM)),
            scratch_shapes=[
                pltpu.VMEM((HEADS, TOK, HEAD), bf16),
                pltpu.VMEM((HEADS, TOK, HEAD), bf16),
                pltpu.VMEM((KV_HEADS, 2 * TOK, HEAD), bf16),
                pltpu.VMEM((KV_HEADS, 2 * TOK, HEAD), bf16),
                pltpu.VMEM((HEADS, TOK, HEAD), bf16),
                pltpu.VMEM((2, KV_HEADS, TOK, HEAD), f32),
                pltpu.VMEM((2, KV_HEADS, TOK, HEAD), bf16),
                pltpu.VMEM((2, KV_HEADS, TOK, HEAD), bf16),
                pltpu.VMEM((2, KV_HEADS, TOK, HEAD), bf16),
                pltpu.VMEM((2 * TOK, TOK), f32),
                pltpu.SMEM((HEADS,), f32),
                pltpu.VMEM((HEADS, TOK), f32),
                pltpu.VMEM((nd, 1, HEAD), f32),
                pltpu.VMEM((nc, 1, HEAD), f32),
                pltpu.SemaphoreType.DMA((2, HEADS)),
                pltpu.SemaphoreType.DMA((KV_HEADS, 2)),
                pltpu.SemaphoreType.DMA,
                pltpu.SemaphoreType.DMA((KV_HEADS, 2)),
                pltpu.SemaphoreType.DMA((KV_HEADS, 2)),
                pltpu.SemaphoreType.DMA((KV_HEADS, 2)),
                pltpu.SemaphoreType.DMA((KV_HEADS, 2)),
                pltpu.SemaphoreType.DMA((HEADS,)),
                pltpu.SemaphoreType.DMA((KV_HEADS, 2)),
                pltpu.SemaphoreType.DMA((2,)),
                pltpu.SemaphoreType.DMA((2,)),
            ],
            compiler_params=pltpu.CompilerParams(collective_id=0, has_side_effects=True),
        )(queries, keys, values, dout, sinks)
        return dq, dk, dv, sg[0, :HEADS]

    tokens = P("dp", "ctx", None)
    return jax.shard_map(
        body,
        mesh=mesh,
        in_specs=(tokens, tokens, tokens, tokens, P()),
        out_specs=(tokens, tokens, tokens, P()),
        check_vma=False,
    )
```

```python
import functools

import jax
import jax.numpy as jnp
from jax import lax
from jax.experimental import pallas as pl
from jax.experimental.pallas import tpu as pltpu
from jax.sharding import PartitionSpec as P

HEADS = 16
KV_HEADS = 4
GROUP = HEADS // KV_HEADS
HEAD = 128
TOK = 128
SCALE = HEAD ** (-0.5)
LOG2E = 1.4426950408889634
MASKED = -1e30
MESH = pl.DeviceIdType.MESH

NT = (((1,), (1,)), ((), ()))
NN = (((1,), (0,)), ((), ()))
TN = (((0,), (0,)), ((), ()))


def dot(a, b, dims):
    return lax.dot_general(a, b, dims, preferred_element_type=jnp.float32)


def remote(src, dst, send, recv, device):
    return pltpu.make_async_remote_copy(
        src_ref=src, dst_ref=dst, send_sem=send, recv_sem=recv, device_id=device, device_id_type=MESH
    )


def cols(h):
    return pl.ds(h * HEAD, HEAD)


def kernel(
    nd, nc, token_root,
    q_hbm, k_hbm, v_hbm, do_hbm, sinks_hbm,
    dq_ref, dk_ref, dv_ref, sg_ref,
    qv, dov, kj, vj, own, back, landed, bias, sinks_s, terms, part_a, part_b,
    in_sem, kv_sem, sink_sem, halo_send, halo_recv, grad_send, grad_recv, sum_send, sum_recv,
):
    d = lax.axis_index("dp")
    c = lax.axis_index("ctx")
    left, right = c - 1, c + 1
    has_left, has_right = c > 0, c < nc - 1

    x_n, y_n, z_n = nc // 4, nd // 4, 8
    x, y, core = c // 4, d // 4, d % 2
    z = (c % 4) * 2 + (d // 2) % 2

    def at(dx, dy, dz, dcore):
        to_x, to_y, to_z, to_core = (x + dx) % x_n, (y + dy) % y_n, (z + dz) % z_n, (core + dcore) % 2
        return to_y * 4 + (to_z % 2) * 2 + to_core, to_x * 4 + to_z // 2

    def hops(n, step):
        return min(step, n - step)

    stage_a = [(0, 0, dz, dcore) for dz in range(z_n) for dcore in range(2)][1:]
    stage_b = [(dx, dy, 0, 0) for dx in range(x_n) for dy in range(y_n)][1:]
    stage_a.sort(key=lambda o: -hops(z_n, o[2]))
    stage_b.sort(key=lambda o: -hops(x_n, o[0]) - hops(y_n, o[1]))

    loads = []
    for g in range(KV_HEADS):
        pairs = [(k_hbm.at[0, :, cols(g)], kj.at[g, pl.ds(TOK, TOK)]), (v_hbm.at[0, :, cols(g)], vj.at[g, pl.ds(TOK, TOK)])]
        loads.append([pltpu.make_async_copy(s, t, kv_sem.at[g, n]) for n, (s, t) in enumerate(pairs)])
        for h in range(g * GROUP, (g + 1) * GROUP):
            loads[g].append(pltpu.make_async_copy(q_hbm.at[0, :, cols(h)], qv.at[h], in_sem.at[0, h]))
            loads[g].append(pltpu.make_async_copy(do_hbm.at[0, :, cols(h)], dov.at[h], in_sem.at[1, h]))
    sink_load = pltpu.make_async_copy(sinks_hbm, sinks_s, sink_sem)
    sink_load.start()
    for group in loads:
        for copy in group:
            copy.start()

    barrier = pltpu.get_barrier_semaphore()

    def greet(device):
        pl.semaphore_signal(barrier, inc=1, device_id=device, device_id_type=MESH)

    @pl.when(has_left)
    def _():
        greet((d, left))

    @pl.when(has_right)
    def _():
        greet((d, right))

    for offset in stage_a + stage_b:
        greet(at(*offset))
    as_int = lambda flag: jnp.where(flag, 1, 0)
    pl.semaphore_wait(barrier, as_int(has_left) + as_int(has_right) + len(stage_a) + len(stage_b))

    halo = []
    for g in range(KV_HEADS):
        for n, (src, dst) in enumerate(((k_hbm, kj), (v_hbm, vj))):
            halo.append(
                remote(src.at[0, :, cols(g)], dst.at[g, pl.ds(0, TOK)], halo_send.at[g, n], halo_recv.at[g, n], (d, right))
            )

    @pl.when(has_right)
    def _():
        for copy in halo:
            copy.start()

    @pl.when(c == 0)
    def _():
        kj[:, 0:TOK] = jnp.zeros((KV_HEADS, TOK, HEAD), jnp.bfloat16)
        vj[:, 0:TOK] = jnp.zeros((KV_HEADS, TOK, HEAD), jnp.bfloat16)

    key = lax.broadcasted_iota(jnp.int32, (TOK, TOK), 0)
    query = lax.broadcasted_iota(jnp.int32, (TOK, TOK), 1)
    first = jnp.where(c == 0, TOK, 0)
    bias[0:TOK] = jnp.where(key > query + first, 0.0, MASKED)
    bias[TOK:] = jnp.where(key <= query, 0.0, MASKED)
    sink_load.wait()

    def sum_stage(n, part, slot, offsets, value):
        part[slot] = value
        for offset in offsets:
            remote(part.at[slot], part.at[slot], sum_send.at[n], sum_recv.at[n], at(*offset)).start()
        if offsets:
            some = part.at[pl.ds(0, len(offsets))]
            return [remote(some, some, sum_send.at[n], sum_recv.at[n], at(*offsets[0]))]
        return []

    grads = []
    for g in range(KV_HEADS):
        for copy in loads[g]:
            copy.wait()

        @pl.when(has_left)
        def _():
            halo[2 * g].wait_recv()
            halo[2 * g + 1].wait_recv()

        heads = pl.ds(g * GROUP, GROUP)
        qs = qv[heads].reshape(GROUP * TOK, HEAD)
        dos = dov[heads].reshape(GROUP * TOK, HEAD)
        kk = kj[g]
        vv = vj[g]
        mask = bias[...]
        mask = jnp.concatenate([mask] * GROUP, axis=1)
        sink = jnp.concatenate(
            [jnp.full((1, TOK), sinks_s[g * GROUP + n] * LOG2E, jnp.float32) for n in range(GROUP)], axis=1
        )
        s = dot(kk, qs, NT) * (SCALE * LOG2E) + mask
        top = jnp.maximum(jnp.max(s, axis=0, keepdims=True), sink)
        e = jnp.exp2(s - top)
        at_sink = jnp.exp2(sink - top)
        inv = 1.0 / (jnp.sum(e, axis=0, keepdims=True) + at_sink)
        p = e * inv
        dp = dot(vv, dos, NT)
        weighted = p * dp
        delta = jnp.sum(weighted, axis=0, keepdims=True)
        term = at_sink * inv * delta
        for n in range(GROUP):
            terms[pl.ds(g * GROUP + n, 1), :] = term[:, n * TOK : (n + 1) * TOK]
        if g == KV_HEADS - 1:
            row = lax.broadcasted_iota(jnp.int32, (HEADS, TOK), 0)
            lane = lax.broadcasted_iota(jnp.int32, (HEADS, TOK), 1)
            sums = jnp.sum(terms[...], axis=1, keepdims=True)
            local = jnp.sum(jnp.where(row == lane, sums, 0.0), axis=0, keepdims=True)
            sent_a = sum_stage(0, part_a, z * 2 + core, stage_a, local)

        ds = (weighted - p * delta).astype(jnp.bfloat16)
        pr = p.astype(jnp.bfloat16)
        dk = dot(ds, qs, NN) * SCALE
        dv = dot(pr, dos, NN)
        back[0, g] = dk[:TOK].astype(jnp.bfloat16)
        back[1, g] = dv[:TOK].astype(jnp.bfloat16)
        own[0, g] = dk[TOK:]
        own[1, g] = dv[TOK:]
        dq = (dot(ds, kk, TN) * SCALE).astype(jnp.bfloat16)
        for n in range(GROUP):
            dq_ref[0, :, cols(g * GROUP + n)] = dq[n * TOK : (n + 1) * TOK]
        for n in range(2):
            grads.append(remote(back.at[n, g], landed.at[n, g], grad_send.at[g, n], grad_recv.at[g, n], (d, left)))

        @pl.when(has_left)
        def _():
            for copy in grads[2 * g :]:
                copy.start()

    for copy in sent_a:
        copy.wait_recv()
    sent_b = sum_stage(1, part_b, x * y_n + y, stage_b, jnp.sum(part_a[...], axis=0))

    for g in range(KV_HEADS):
        for n, out in enumerate((dk_ref, dv_ref)):

            @pl.when(has_right)
            def _():
                grads[2 * g + n].wait_recv()
                out[0, :, cols(g)] = (own[n, g] + landed[n, g].astype(jnp.float32)).astype(jnp.bfloat16)

            @pl.when(c == nc - 1)
            def _():
                out[0, :, cols(g)] = own[n, g].astype(jnp.bfloat16)

    for copy in sent_b:
        copy.wait_recv()
    sg_ref[...] = jnp.sum(part_b[...], axis=0) * (-1.0 / token_root)

    @pl.when(has_right)
    def _():
        for copy in halo:
            copy.wait_send()

    @pl.when(has_left)
    def _():
        for copy in grads:
            copy.wait_send()

    for copy in sent_a + sent_b:
        copy.wait_send()


def write_kernel(dq_ref, dk_ref, dv_ref, sg_ref, dq_out, dk_out, dv_out, sg_out, sem):
    pairs = ((dq_ref, dq_out), (dk_ref, dk_out), (dv_ref, dv_out))
    copies = [pltpu.make_async_copy(src, dst, sem.at[n]) for n, (src, dst) in enumerate(pairs)]
    for copy in copies:
        copy.start()
    sg_out[...] = sg_ref[0, :HEADS]
    for copy in copies:
        copy.wait()


def solution(mesh):
    nd, nc = mesh.shape["dp"], mesh.shape["ctx"]
    any_space = pl.BlockSpec(memory_space=pl.ANY)
    vmem_space = pl.BlockSpec(memory_space=pltpu.VMEM)

    def body(queries, keys, values, dout, sinks):
        token_root = float(nd * queries.shape[0] * nc * queries.shape[1]) ** 0.5
        bf16, f32 = jnp.bfloat16, jnp.float32
        results = pl.pallas_call(
            functools.partial(kernel, nd, nc, token_root),
            out_shape=(
                pltpu.VMEM(queries.shape, bf16),
                pltpu.VMEM(keys.shape, bf16),
                pltpu.VMEM(values.shape, bf16),
                pltpu.VMEM((1, HEAD), f32),
            ),
            in_specs=[any_space] * 5,
            out_specs=(vmem_space,) * 4,
            scratch_shapes=[
                pltpu.VMEM((HEADS, TOK, HEAD), bf16),
                pltpu.VMEM((HEADS, TOK, HEAD), bf16),
                pltpu.VMEM((KV_HEADS, 2 * TOK, HEAD), bf16),
                pltpu.VMEM((KV_HEADS, 2 * TOK, HEAD), bf16),
                pltpu.VMEM((2, KV_HEADS, TOK, HEAD), f32),
                pltpu.VMEM((2, KV_HEADS, TOK, HEAD), bf16),
                pltpu.VMEM((2, KV_HEADS, TOK, HEAD), bf16),
                pltpu.VMEM((2 * TOK, TOK), f32),
                pltpu.SMEM((HEADS,), f32),
                pltpu.VMEM((HEADS, TOK), f32),
                pltpu.VMEM((16, 1, HEAD), f32),
                pltpu.VMEM((nd * nc // 16, 1, HEAD), f32),
                pltpu.SemaphoreType.DMA((2, HEADS)),
                pltpu.SemaphoreType.DMA((KV_HEADS, 2)),
                pltpu.SemaphoreType.DMA,
                pltpu.SemaphoreType.DMA((KV_HEADS, 2)),
                pltpu.SemaphoreType.DMA((KV_HEADS, 2)),
                pltpu.SemaphoreType.DMA((KV_HEADS, 2)),
                pltpu.SemaphoreType.DMA((KV_HEADS, 2)),
                pltpu.SemaphoreType.DMA((2,)),
                pltpu.SemaphoreType.DMA((2,)),
            ],
            compiler_params=pltpu.CompilerParams(collective_id=0, has_side_effects=True),
        )(queries, keys, values, dout, sinks)
        return pl.pallas_call(
            write_kernel,
            out_shape=(
                jax.ShapeDtypeStruct(queries.shape, bf16),
                jax.ShapeDtypeStruct(keys.shape, bf16),
                jax.ShapeDtypeStruct(values.shape, bf16),
                jax.ShapeDtypeStruct((HEADS,), f32),
            ),
            in_specs=[vmem_space] * 4,
            out_specs=(any_space, any_space, any_space, vmem_space),
            scratch_shapes=[pltpu.SemaphoreType.DMA((3,))],
            compiler_params=pltpu.CompilerParams(vmem_limit_bytes=1 << 20),
        )(*results)

    tokens = P("dp", "ctx", None)
    return jax.shard_map(
        body,
        mesh=mesh,
        in_specs=(tokens, tokens, tokens, tokens, P()),
        out_specs=(tokens, tokens, tokens, P()),
        check_vma=False,
    )
```

```python
import functools

import jax
import jax.numpy as jnp
from jax import lax
from jax.experimental import pallas as pl
from jax.experimental.pallas import tpu as pltpu
from jax.sharding import PartitionSpec as P

HEADS = 16
KV_HEADS = 4
GROUP = HEADS // KV_HEADS
HEAD = 128
TOK = 128
SCALE = HEAD ** (-0.5)
LOG2E = 1.4426950408889634
MASKED = -1e30
MESH = pl.DeviceIdType.MESH

NT = (((1,), (1,)), ((), ()))
NN = (((1,), (0,)), ((), ()))
TN = (((0,), (0,)), ((), ()))


def dot(a, b, dims):
    return lax.dot_general(a, b, dims, preferred_element_type=jnp.float32)


def remote(src, dst, send, recv, device):
    return pltpu.make_async_remote_copy(
        src_ref=src, dst_ref=dst, send_sem=send, recv_sem=recv, device_id=device, device_id_type=MESH
    )


def cols(h):
    return pl.ds(h * HEAD, HEAD)


def kernel(
    nd, nc, token_root,
    q_hbm, k_hbm, v_hbm, do_hbm, sinks_hbm,
    dq_ref, dk_ref, dv_ref, sg_ref,
    qv, dov, kv, prior, own, back, landed, bias, sinks_s, terms, part_a, part_b,
    in_sem, kv_sem, sink_sem, halo_send, halo_recv, grad_send, grad_recv, sum_send, sum_recv,
):
    d = lax.axis_index("dp")
    c = lax.axis_index("ctx")
    left, right = c - 1, c + 1
    has_left, has_right = c > 0, c < nc - 1

    x_n, y_n, z_n = nc // 4, nd // 4, 8
    x, y, core = c // 4, d // 4, d % 2
    z = (c % 4) * 2 + (d // 2) % 2

    def at(dx, dy, dz, dcore):
        to_x, to_y, to_z, to_core = (x + dx) % x_n, (y + dy) % y_n, (z + dz) % z_n, (core + dcore) % 2
        return to_y * 4 + (to_z % 2) * 2 + to_core, to_x * 4 + to_z // 2

    def hops(n, step):
        return min(step, n - step)

    stage_a = [(dx, 0, 0, dc) for dx in range(x_n) for dc in range(2)][1:]
    stage_b = [(0, dy, dz, 0) for dy in range(y_n) for dz in range(z_n)][1:]
    far = lambda o: -hops(x_n, o[0]) - hops(y_n, o[1]) - hops(z_n, o[2])
    stage_a.sort(key=far)
    stage_b.sort(key=far)

    barrier = pltpu.get_barrier_semaphore()

    def greet(device):
        pl.semaphore_signal(barrier, inc=1, device_id=device, device_id_type=MESH)

    @pl.when(has_left)
    def _():
        greet((d, left))

    @pl.when(has_right)
    def _():
        greet((d, right))

    for offset in stage_a + stage_b:
        greet(at(*offset))

    sink_load = pltpu.make_async_copy(sinks_hbm, sinks_s, sink_sem)
    own_loads = [pltpu.make_async_copy(src.at[0], dst, kv_sem.at[n]) for n, (src, dst) in enumerate(((k_hbm, kv.at[0]), (v_hbm, kv.at[1])))]
    loads = [
        [
            pltpu.make_async_copy(src.at[0, :, pl.ds(g * GROUP * HEAD, GROUP * HEAD)], dst.at[g], in_sem.at[n, g])
            for n, (src, dst) in enumerate(((q_hbm, qv), (do_hbm, dov)))
        ]
        for g in range(KV_HEADS)
    ]
    for copy in [sink_load, *own_loads, *sum(loads, [])]:
        copy.start()

    as_int = lambda flag: jnp.where(flag, 1, 0)
    pl.semaphore_wait(barrier, as_int(has_left) + as_int(has_right) + len(stage_a) + len(stage_b))

    halo = []
    for g in range(KV_HEADS):
        for n, src in enumerate((k_hbm, v_hbm)):
            halo.append(
                remote(src.at[0, :, cols(g)], prior.at[n, g], halo_send.at[g, n], halo_recv.at[g, n], (d, right))
            )

    @pl.when(has_right)
    def _():
        for copy in halo:
            copy.start()

    @pl.when(c == 0)
    def _():
        prior[...] = jnp.zeros((2, KV_HEADS, TOK, HEAD), jnp.bfloat16)

    key = lax.broadcasted_iota(jnp.int32, (TOK, TOK), 0)
    query = lax.broadcasted_iota(jnp.int32, (TOK, TOK), 1)
    first = jnp.where(c == 0, TOK, 0)
    bias[0:TOK] = jnp.where(key > query + first, 0.0, MASKED)
    bias[TOK:] = jnp.where(key <= query, 0.0, MASKED)
    for copy in [sink_load, *own_loads]:
        copy.wait()

    def sum_stage(n, part, slot, offsets, value):
        part[slot] = value
        for offset in offsets:
            remote(part.at[slot], part.at[slot], sum_send.at[n], sum_recv.at[n], at(*offset)).start()
        if offsets:
            some = part.at[pl.ds(0, len(offsets))]
            return [remote(some, some, sum_send.at[n], sum_recv.at[n], at(*offsets[0]))]
        return []

    grads = []
    for g in range(KV_HEADS):
        for copy in loads[g]:
            copy.wait()

        def stacked(ref):
            return jnp.concatenate([ref[g, :, cols(n)] for n in range(GROUP)], axis=0)

        def joined(n):
            @pl.when(has_left)
            def _():
                halo[2 * g + n].wait_recv()

            return jnp.concatenate([prior[n, g], kv[n, :, cols(g)]], axis=0)

        qs = stacked(qv)
        dos = stacked(dov)
        kk = joined(0)
        mask = bias[...]
        mask = jnp.concatenate([mask] * GROUP, axis=1)
        sink = jnp.concatenate(
            [jnp.full((1, TOK), sinks_s[g * GROUP + n] * LOG2E, jnp.float32) for n in range(GROUP)], axis=1
        )
        s = dot(kk, qs, NT) * (SCALE * LOG2E) + mask
        top = jnp.maximum(jnp.max(s, axis=0, keepdims=True), sink)
        e = jnp.exp2(s - top)
        at_sink = jnp.exp2(sink - top)
        inv = 1.0 / (jnp.sum(e, axis=0, keepdims=True) + at_sink)
        p = e * inv
        vv = joined(1)
        dp = dot(vv, dos, NT)
        weighted = p * dp
        delta = jnp.sum(weighted, axis=0, keepdims=True)
        term = at_sink * inv * delta
        for n in range(GROUP):
            terms[pl.ds(g * GROUP + n, 1), :] = term[:, n * TOK : (n + 1) * TOK]
        if g == KV_HEADS - 1:
            row = lax.broadcasted_iota(jnp.int32, (HEADS, TOK), 0)
            lane = lax.broadcasted_iota(jnp.int32, (HEADS, TOK), 1)
            sums = jnp.sum(terms[...], axis=1, keepdims=True)
            local = jnp.sum(jnp.where(row == lane, sums, 0.0), axis=0, keepdims=True)
            sent_a = sum_stage(0, part_a, x * 2 + core, stage_a, local)

        ds = (weighted - p * delta).astype(jnp.bfloat16)
        pr = p.astype(jnp.bfloat16)
        dk = dot(ds, qs, NN) * SCALE
        dv = dot(pr, dos, NN)
        back[0, g] = dk[:TOK].astype(jnp.bfloat16)
        back[1, g] = dv[:TOK].astype(jnp.bfloat16)
        own[0, g] = dk[TOK:]
        own[1, g] = dv[TOK:]
        dq = (dot(ds, kk, TN) * SCALE).astype(jnp.bfloat16)
        for n in range(GROUP):
            dq_ref[0, :, cols(g * GROUP + n)] = dq[n * TOK : (n + 1) * TOK]
        for n in range(2):
            grads.append(remote(back.at[n, g], landed.at[n, g], grad_send.at[g, n], grad_recv.at[g, n], (d, left)))

        @pl.when(has_left)
        def _():
            for copy in grads[2 * g :]:
                copy.start()

    for copy in sent_a:
        copy.wait_recv()
    sent_b = sum_stage(1, part_b, y * z_n + z, stage_b, jnp.sum(part_a[...], axis=0))

    for g in range(KV_HEADS):
        for n, out in enumerate((dk_ref, dv_ref)):

            @pl.when(has_right)
            def _():
                grads[2 * g + n].wait_recv()
                out[0, :, cols(g)] = (own[n, g] + landed[n, g].astype(jnp.float32)).astype(jnp.bfloat16)

            @pl.when(c == nc - 1)
            def _():
                out[0, :, cols(g)] = own[n, g].astype(jnp.bfloat16)

    for copy in sent_b:
        copy.wait_recv()
    sg_ref[...] = jnp.sum(part_b[...], axis=0) * (-1.0 / token_root)

    @pl.when(has_right)
    def _():
        for copy in halo:
            copy.wait_send()

    @pl.when(has_left)
    def _():
        for copy in grads:
            copy.wait_send()

    for copy in sent_a + sent_b:
        copy.wait_send()


def write_kernel(dq_ref, dk_ref, dv_ref, sg_ref, dq_out, dk_out, dv_out, sg_out, sg_row, sem):
    sg_row[...] = sg_ref[0, :HEADS]
    rows = [pl.ds(n * TOK // 4, TOK // 4) for n in range(4)]
    pairs = [(dq_ref.at[0, r], dq_out.at[0, r]) for r in rows] + [(dk_ref, dk_out), (dv_ref, dv_out), (sg_row, sg_out)]
    copies = [pltpu.make_async_copy(src, dst, sem.at[n]) for n, (src, dst) in enumerate(pairs)]
    for copy in copies:
        copy.start()
    for copy in copies:
        copy.wait()


def solution(mesh):
    nd, nc = mesh.shape["dp"], mesh.shape["ctx"]
    any_space = pl.BlockSpec(memory_space=pl.ANY)
    vmem_space = pl.BlockSpec(memory_space=pltpu.VMEM)

    def body(queries, keys, values, dout, sinks):
        token_root = float(nd * queries.shape[0] * nc * queries.shape[1]) ** 0.5
        bf16, f32 = jnp.bfloat16, jnp.float32
        results = pl.pallas_call(
            functools.partial(kernel, nd, nc, token_root),
            out_shape=(
                pltpu.VMEM(queries.shape, bf16),
                pltpu.VMEM(keys.shape, bf16),
                pltpu.VMEM(values.shape, bf16),
                pltpu.VMEM((1, HEAD), f32),
            ),
            in_specs=[any_space] * 5,
            out_specs=(vmem_space,) * 4,
            scratch_shapes=[
                pltpu.VMEM((KV_HEADS, TOK, GROUP * HEAD), bf16),
                pltpu.VMEM((KV_HEADS, TOK, GROUP * HEAD), bf16),
                pltpu.VMEM((2, TOK, KV_HEADS * HEAD), bf16),
                pltpu.VMEM((2, KV_HEADS, TOK, HEAD), bf16),
                pltpu.VMEM((2, KV_HEADS, TOK, HEAD), f32),
                pltpu.VMEM((2, KV_HEADS, TOK, HEAD), bf16),
                pltpu.VMEM((2, KV_HEADS, TOK, HEAD), bf16),
                pltpu.VMEM((2 * TOK, TOK), f32),
                pltpu.SMEM((HEADS,), f32),
                pltpu.VMEM((HEADS, TOK), f32),
                pltpu.VMEM((nc // 2, 1, HEAD), f32),
                pltpu.VMEM((nd * 2, 1, HEAD), f32),
                pltpu.SemaphoreType.DMA((2, KV_HEADS)),
                pltpu.SemaphoreType.DMA((2,)),
                pltpu.SemaphoreType.DMA,
                pltpu.SemaphoreType.DMA((KV_HEADS, 2)),
                pltpu.SemaphoreType.DMA((KV_HEADS, 2)),
                pltpu.SemaphoreType.DMA((KV_HEADS, 2)),
                pltpu.SemaphoreType.DMA((KV_HEADS, 2)),
                pltpu.SemaphoreType.DMA((2,)),
                pltpu.SemaphoreType.DMA((2,)),
            ],
            compiler_params=pltpu.CompilerParams(collective_id=0, has_side_effects=True),
        )(queries, keys, values, dout, sinks)
        return pl.pallas_call(
            write_kernel,
            out_shape=(
                jax.ShapeDtypeStruct(queries.shape, bf16),
                jax.ShapeDtypeStruct(keys.shape, bf16),
                jax.ShapeDtypeStruct(values.shape, bf16),
                jax.ShapeDtypeStruct((HEADS,), f32),
            ),
            in_specs=[vmem_space] * 4,
            out_specs=(any_space,) * 4,
            scratch_shapes=[pltpu.VMEM((HEADS,), f32), pltpu.SemaphoreType.DMA((7,))],
            compiler_params=pltpu.CompilerParams(vmem_limit_bytes=1 << 20),
        )(*results)

    tokens = P("dp", "ctx", None)
    return jax.shard_map(
        body,
        mesh=mesh,
        in_specs=(tokens, tokens, tokens, tokens, P()),
        out_specs=(tokens, tokens, tokens, P()),
        check_vma=False,
    )
```

```python
import functools

import jax
import jax.numpy as jnp
from jax import lax
from jax.experimental import pallas as pl
from jax.experimental.pallas import tpu as pltpu
from jax.sharding import PartitionSpec as P

HEADS = 16
KV_HEADS = 4
GROUP = HEADS // KV_HEADS
HEAD = 128
TOK = 128
SCALE = HEAD ** (-0.5)
LOG2E = 1.4426950408889634
MASKED = -1e30
MESH = pl.DeviceIdType.MESH

NT = (((1,), (1,)), ((), ()))
NN = (((1,), (0,)), ((), ()))
TN = (((0,), (0,)), ((), ()))


def dot(a, b, dims):
    return lax.dot_general(a, b, dims, preferred_element_type=jnp.float32)


def remote(src, dst, send, recv, device):
    return pltpu.make_async_remote_copy(
        src_ref=src, dst_ref=dst, send_sem=send, recv_sem=recv, device_id=device, device_id_type=MESH
    )


def cols(h):
    return pl.ds(h * HEAD, HEAD)


def kernel(
    nd, nc, token_root,
    q_hbm, k_hbm, v_hbm, do_hbm, sinks_hbm,
    dq_ref, dk_ref, dv_ref, sg_ref,
    qv, dov, kv, prior, own, back, landed, bias, sinks_s, terms, part_a, part_b,
    in_sem, kv_sem, sink_sem, halo_send, halo_recv, grad_send, grad_recv, sum_send, sum_recv, round_sem,
):
    d = lax.axis_index("dp")
    c = lax.axis_index("ctx")
    left, right = c - 1, c + 1
    has_left, has_right = c > 0, c < nc - 1

    x_n, y_n, z_n = nc // 4, nd // 4, 8
    x, y, core = c // 4, d // 4, d % 2
    z = (c % 4) * 2 + (d // 2) % 2

    def at(dx, dy, dz, dcore):
        to_x, to_y, to_z, to_core = (x + dx) % x_n, (y + dy) % y_n, (z + dz) % z_n, (core + dcore) % 2
        return to_y * 4 + (to_z % 2) * 2 + to_core, to_x * 4 + to_z // 2

    def hops(n, step):
        return min(step, n - step)

    stage_a = [(dx, 0, 0, dc) for dx in range(x_n) for dc in range(2)][1:]
    stage_b = [(0, dy, dz, 0) for dy in range(y_n) for dz in range(z_n)][1:]
    far = lambda o: -hops(x_n, o[0]) - hops(y_n, o[1]) - hops(z_n, o[2])
    stage_a.sort(key=far)
    stage_b.sort(key=far)

    half = y_n // 2
    near = [(0, 0, 1, 0), (0, 0, z_n - 1, 0), (0, 1, 0, 0), (0, y_n - 1, 0, 0)]
    twice = [(0, 0, 2, 0), (0, 0, z_n - 2, 0), (0, 2, 0, 0), (0, y_n - 2, 0, 0)]
    corner = [(0, dy, dz, 0) for dy in (2, y_n - 2) for dz in (2, z_n - 2)]
    rounds = [near, near + twice, [(0, 0, z_n // 2, 0), (0, half, 0, 0)] + corner]

    barrier = pltpu.get_barrier_semaphore()

    def greet(device):
        pl.semaphore_signal(barrier, inc=1, device_id=device, device_id_type=MESH)

    @pl.when(has_left)
    def _():
        greet((d, left))

    @pl.when(has_right)
    def _():
        greet((d, right))

    for offset in stage_a + near:
        greet(at(*offset))

    sink_load = pltpu.make_async_copy(sinks_hbm, sinks_s, sink_sem)
    own_loads = [pltpu.make_async_copy(src.at[0], dst, kv_sem.at[n]) for n, (src, dst) in enumerate(((k_hbm, kv.at[0]), (v_hbm, kv.at[1])))]
    loads = [
        [
            pltpu.make_async_copy(src.at[0, :, pl.ds(g * GROUP * HEAD, GROUP * HEAD)], dst.at[g], in_sem.at[n, g])
            for n, (src, dst) in enumerate(((q_hbm, qv), (do_hbm, dov)))
        ]
        for g in range(KV_HEADS)
    ]
    for copy in [sink_load, *own_loads, *sum(loads, [])]:
        copy.start()

    as_int = lambda flag: jnp.where(flag, 1, 0)
    pl.semaphore_wait(barrier, as_int(has_left) + as_int(has_right) + len(stage_a) + len(near))

    halo = []
    for g in range(KV_HEADS):
        for n, src in enumerate((k_hbm, v_hbm)):
            halo.append(
                remote(src.at[0, :, cols(g)], prior.at[n, g], halo_send.at[g, n], halo_recv.at[g, n], (d, right))
            )

    @pl.when(has_right)
    def _():
        for copy in halo:
            copy.start()

    @pl.when(c == 0)
    def _():
        prior[...] = jnp.zeros((2, KV_HEADS, TOK, HEAD), jnp.bfloat16)

    key = lax.broadcasted_iota(jnp.int32, (TOK, TOK), 0)
    query = lax.broadcasted_iota(jnp.int32, (TOK, TOK), 1)
    first = jnp.where(c == 0, TOK, 0)
    bias[0:TOK] = jnp.where(key > query + first, 0.0, MASKED)
    bias[TOK:] = jnp.where(key <= query, 0.0, MASKED)
    for copy in [sink_load, *own_loads]:
        copy.wait()

    def sum_stage(n, part, slot, offsets, value):
        part[slot] = value
        for offset in offsets:
            remote(part.at[slot], part.at[slot], sum_send.at[n], sum_recv.at[n], at(*offset)).start()
        if offsets:
            some = part.at[pl.ds(0, len(offsets))]
            return [remote(some, some, sum_send.at[n], sum_recv.at[n], at(*offsets[0]))]
        return []

    for n, offsets in enumerate(rounds):
        for offset in offsets:
            pl.semaphore_signal(round_sem.at[n], inc=1, device_id=at(*offset), device_id_type=MESH)
        pl.semaphore_wait(round_sem.at[n], len(offsets))

    grads = []
    for g in range(KV_HEADS):
        for copy in loads[g]:
            copy.wait()

        def stacked(ref):
            return jnp.concatenate([ref[g, :, cols(n)] for n in range(GROUP)], axis=0)

        def joined(n):
            @pl.when(has_left)
            def _():
                halo[2 * g + n].wait_recv()

            return jnp.concatenate([prior[n, g], kv[n, :, cols(g)]], axis=0)

        qs = stacked(qv)
        dos = stacked(dov)
        kk = joined(0)
        mask = bias[...]
        mask = jnp.concatenate([mask] * GROUP, axis=1)
        sink = jnp.concatenate(
            [jnp.full((1, TOK), sinks_s[g * GROUP + n] * LOG2E, jnp.float32) for n in range(GROUP)], axis=1
        )
        s = dot(kk, qs, NT) * (SCALE * LOG2E) + mask
        top = jnp.maximum(jnp.max(s, axis=0, keepdims=True), sink)
        e = jnp.exp2(s - top)
        at_sink = jnp.exp2(sink - top)
        inv = 1.0 / (jnp.sum(e, axis=0, keepdims=True) + at_sink)
        p = e * inv
        vv = joined(1)
        dp = dot(vv, dos, NT)
        weighted = p * dp
        delta = jnp.sum(weighted, axis=0, keepdims=True)
        term = at_sink * inv * delta
        for n in range(GROUP):
            terms[pl.ds(g * GROUP + n, 1), :] = term[:, n * TOK : (n + 1) * TOK]
        if g == KV_HEADS - 1:
            row = lax.broadcasted_iota(jnp.int32, (HEADS, TOK), 0)
            lane = lax.broadcasted_iota(jnp.int32, (HEADS, TOK), 1)
            sums = jnp.sum(terms[...], axis=1, keepdims=True)
            local = jnp.sum(jnp.where(row == lane, sums, 0.0), axis=0, keepdims=True)
            sent_a = sum_stage(0, part_a, x * 2 + core, stage_a, local)

        ds = (weighted - p * delta).astype(jnp.bfloat16)
        pr = p.astype(jnp.bfloat16)
        dk = dot(ds, qs, NN) * SCALE
        dv = dot(pr, dos, NN)
        back[0, g] = dk[:TOK].astype(jnp.bfloat16)
        back[1, g] = dv[:TOK].astype(jnp.bfloat16)
        own[0, g] = dk[TOK:]
        own[1, g] = dv[TOK:]
        dq = (dot(ds, kk, TN) * SCALE).astype(jnp.bfloat16)
        for n in range(GROUP):
            dq_ref[0, :, cols(g * GROUP + n)] = dq[n * TOK : (n + 1) * TOK]
        for n in range(2):
            grads.append(remote(back.at[n, g], landed.at[n, g], grad_send.at[g, n], grad_recv.at[g, n], (d, left)))

        @pl.when(has_left)
        def _():
            for copy in grads[2 * g :]:
                copy.start()

    for copy in sent_a:
        copy.wait_recv()
    sent_b = sum_stage(1, part_b, y * z_n + z, stage_b, jnp.sum(part_a[...], axis=0))

    for g in range(KV_HEADS):
        for n, out in enumerate((dk_ref, dv_ref)):

            @pl.when(has_right)
            def _():
                grads[2 * g + n].wait_recv()
                out[0, :, cols(g)] = (own[n, g] + landed[n, g].astype(jnp.float32)).astype(jnp.bfloat16)

            @pl.when(c == nc - 1)
            def _():
                out[0, :, cols(g)] = own[n, g].astype(jnp.bfloat16)

    for copy in sent_b:
        copy.wait_recv()
    sg_ref[...] = jnp.sum(part_b[...], axis=0) * (-1.0 / token_root)

    @pl.when(has_right)
    def _():
        for copy in halo:
            copy.wait_send()

    @pl.when(has_left)
    def _():
        for copy in grads:
            copy.wait_send()

    for copy in sent_a + sent_b:
        copy.wait_send()


def write_kernel(dq_ref, dk_ref, dv_ref, sg_ref, dq_out, dk_out, dv_out, sg_out, sg_row, sem):
    sg_row[...] = sg_ref[0, :HEADS]
    rows = [pl.ds(n * TOK // 4, TOK // 4) for n in range(4)]
    pairs = [(dq_ref.at[0, r], dq_out.at[0, r]) for r in rows] + [(dk_ref, dk_out), (dv_ref, dv_out), (sg_row, sg_out)]
    copies = [pltpu.make_async_copy(src, dst, sem.at[n]) for n, (src, dst) in enumerate(pairs)]
    for copy in copies:
        copy.start()
    for copy in copies:
        copy.wait()


def solution(mesh):
    nd, nc = mesh.shape["dp"], mesh.shape["ctx"]
    any_space = pl.BlockSpec(memory_space=pl.ANY)
    vmem_space = pl.BlockSpec(memory_space=pltpu.VMEM)

    def body(queries, keys, values, dout, sinks):
        token_root = float(nd * queries.shape[0] * nc * queries.shape[1]) ** 0.5
        bf16, f32 = jnp.bfloat16, jnp.float32
        results = pl.pallas_call(
            functools.partial(kernel, nd, nc, token_root),
            out_shape=(
                pltpu.VMEM(queries.shape, bf16),
                pltpu.VMEM(keys.shape, bf16),
                pltpu.VMEM(values.shape, bf16),
                pltpu.VMEM((1, HEAD), f32),
            ),
            in_specs=[any_space] * 5,
            out_specs=(vmem_space,) * 4,
            scratch_shapes=[
                pltpu.VMEM((KV_HEADS, TOK, GROUP * HEAD), bf16),
                pltpu.VMEM((KV_HEADS, TOK, GROUP * HEAD), bf16),
                pltpu.VMEM((2, TOK, KV_HEADS * HEAD), bf16),
                pltpu.VMEM((2, KV_HEADS, TOK, HEAD), bf16),
                pltpu.VMEM((2, KV_HEADS, TOK, HEAD), f32),
                pltpu.VMEM((2, KV_HEADS, TOK, HEAD), bf16),
                pltpu.VMEM((2, KV_HEADS, TOK, HEAD), bf16),
                pltpu.VMEM((2 * TOK, TOK), f32),
                pltpu.SMEM((HEADS,), f32),
                pltpu.VMEM((HEADS, TOK), f32),
                pltpu.VMEM((nc // 2, 1, HEAD), f32),
                pltpu.VMEM((nd * 2, 1, HEAD), f32),
                pltpu.SemaphoreType.DMA((2, KV_HEADS)),
                pltpu.SemaphoreType.DMA((2,)),
                pltpu.SemaphoreType.DMA,
                pltpu.SemaphoreType.DMA((KV_HEADS, 2)),
                pltpu.SemaphoreType.DMA((KV_HEADS, 2)),
                pltpu.SemaphoreType.DMA((KV_HEADS, 2)),
                pltpu.SemaphoreType.DMA((KV_HEADS, 2)),
                pltpu.SemaphoreType.DMA((2,)),
                pltpu.SemaphoreType.DMA((2,)),
                pltpu.SemaphoreType.REGULAR((3,)),
            ],
            compiler_params=pltpu.CompilerParams(collective_id=0, has_side_effects=True),
        )(queries, keys, values, dout, sinks)
        return pl.pallas_call(
            write_kernel,
            out_shape=(
                jax.ShapeDtypeStruct(queries.shape, bf16),
                jax.ShapeDtypeStruct(keys.shape, bf16),
                jax.ShapeDtypeStruct(values.shape, bf16),
                jax.ShapeDtypeStruct((HEADS,), f32),
            ),
            in_specs=[vmem_space] * 4,
            out_specs=(any_space,) * 4,
            scratch_shapes=[pltpu.VMEM((HEADS,), f32), pltpu.SemaphoreType.DMA((7,))],
            compiler_params=pltpu.CompilerParams(vmem_limit_bytes=1 << 20),
        )(*results)

    tokens = P("dp", "ctx", None)
    return jax.shard_map(
        body,
        mesh=mesh,
        in_specs=(tokens, tokens, tokens, tokens, P()),
        out_specs=(tokens, tokens, tokens, P()),
        check_vma=False,
    )
```
